256 devices in a mesh: seq: 32 (over x, y, core), tensor: 8 (over z).
Axes of the slice: x: 4, y: 4, z: 8, core: 2. Of those that a mesh axis runs over, the one named last changes fastest.
Arguments:
- tokens: bfloat16 [4, 4, 1600], replicated, may hold values from -6 to 6
- first_gain: float32 [1600], replicated, may hold values from 0.25 to 1.75
- first_shift: float32 [1600], replicated, may hold values from -3 to 3
- input_weight: bfloat16 [1600, 3, 2048], P(None, None, 'tensor'), may hold values from -0.15625 to 0.15625
- input_bias: float32 [3, 2048], P(None, 'tensor')
- output_weight: bfloat16 [2048, 1600], P('tensor'), may hold values from -0.125 to 0.125
- output_bias: float32 [1600], replicated, may hold values from -3 to 3
- second_gain: float32 [1600], replicated, may hold values from 0.25 to 1.75
- second_shift: float32 [1600], replicated, may hold values from -3 to 3
- expand_weight: bfloat16 [1600, 6400], P(None, 'tensor'), may hold values from -0.15625 to 0.15625
- expand_bias: float32 [6400], P('tensor'), may hold values from -3 to 3
- contract_weight: bfloat16 [6400, 1600], P('tensor'), may hold values from -0.078125 to 0.078125
- contract_bias: float32 [1600], replicated, may hold values from -3 to 3
- key_cache: bfloat16 [4, 16384, 2048], P(None, 'seq', 'tensor')
- value_cache: bfloat16 [4, 16384, 2048], P(None, 'seq', 'tensor'), may hold values from -6 to 6
- cache_fill: int32 [4, 32], replicated, may hold values from 0 to 508, as said below
- owner_shard: int32 [4, 4], replicated, may hold values from 0 to 31, as said below
Outputs:
- hidden_out: bfloat16 [4, 4, 1600], replicated
- new_keys: bfloat16 [4, 16384, 2048], P(None, 'seq', 'tensor')
- new_values: bfloat16 [4, 16384, 2048], P(None, 'seq', 'tensor')
The draws below stay inside these ranges and needn't reach their ends.
Inputs may be any that keep to these rules, and one draw needn't show every extreme that they name: `cache_fill`: 1 request hold 506 to 508 entries on every shard; every other request holds 1 to 508 entries on one shard and none on the others. `owner_shard`: a request with entries on one shard only appends all its new tokens to that shard.
All inputs are finite; a program needn't handle non-finite values.
Results may differ from the reference program's by a relative error of at most 0.0046.
Values sent between devices are 32-bit elements; how exact they have to be, the bound alone decides.
A program may use at most 64 MiB of HBM per device.

```python
import math
import jax
import jax.numpy as jnp
from jax import lax

D = 1600
FF = 6400
HEAD_DIM = 64
HEADS = 32
STEPS = 4
B = 4
SEQ_DEV = 512
NS = 16384
HD = 2048


def layout(key):
    order = jax.random.permutation(jax.random.fold_in(key, 11), B)
    longer = order < B // 4
    first_long = order == 0
    home = jax.random.randint(jax.random.fold_in(key, 12), (B,), 0, NS // SEQ_DEV)
    return (longer, first_long, home)


def draw_cache_fill(key, part):
    longer, first_long, home = layout(key)
    shard_count = NS // SEQ_DEV
    columns = lax.iota(jnp.int32, shard_count)[None, :]
    long_fill = SEQ_DEV - STEPS - jax.random.randint(jax.random.fold_in(key, 13), (B, shard_count), 0, 3)
    short_amount = jax.random.randint(jax.random.fold_in(key, 14), (B,), 1, SEQ_DEV - STEPS + 1)
    short_fill = jnp.where(columns == home[:, None], short_amount[:, None], 0)
    filled = jnp.where(longer[:, None], long_fill, short_fill)
    filled = jnp.where(first_long[:, None] & (columns == 0), SEQ_DEV - STEPS, filled)
    return filled.astype(jnp.int32)


def draw_owner_shard(key, part):
    longer, first_long, home = layout(key)
    shard_count = NS // SEQ_DEV
    picks = jax.random.randint(jax.random.fold_in(key, 15), (STEPS, B), 0, shard_count)
    chosen = jnp.where(longer[None, :], picks, home[None, :])
    step_rows = lax.iota(jnp.int32, STEPS)[:, None]
    chosen = jnp.where(first_long[None, :] & (step_rows == 0), shard_count - 1, chosen)
    chosen = jnp.where(first_long[None, :] & (step_rows == 1), 0, chosen)
    return chosen.astype(jnp.int32)


def draw_input_bias(key, part):
    width = HEADS * HEAD_DIM
    return 0.5 * jax.random.normal(jax.random.fold_in(key, 22), (3, width), jnp.float32)


def draw_key_cache(key, part):
    width = HEADS * HEAD_DIM
    drawn = jnp.clip(jax.random.normal(jax.random.fold_in(key, 23), (B, NS, width), jnp.float32), -6.0, 6.0)
    return drawn.astype(jnp.bfloat16)


def steps_of(key, dims, cuts, smallest, high):
    def one(axis_at, blocks):
        heights = jax.random.uniform(jax.random.fold_in(jax.random.fold_in(key, 6), axis_at), (blocks,), jnp.float32, smallest / len(cuts), high / len(cuts))
        return jnp.repeat(jnp.exp(heights), dims[axis_at] // blocks).reshape((-1,) + (1,) * (len(dims) - axis_at - 1))

    level = one(*cuts[0])
    for cut in cuts[1:]:
        level = level * one(*cut)
    return level


def scatter_about(rng, dims, deviation, most, shards=(), kind=jnp.bfloat16):
    values = deviation * jax.random.normal(rng, dims, jnp.float32)
    if shards:
        values = values * steps_of(rng, dims, shards, -0.22, 0.18)
    return jnp.clip(values, -most, most).astype(kind)


def setup_inputs(seed: int = 0) -> dict:
    streams_of = jax.random.split(jax.random.key(seed), 18)
    tokens = scatter_about(streams_of[0], (STEPS, B, D), 1.0, 6.0)
    first_gain = jnp.clip(1.0 + 0.15 * jax.random.normal(streams_of[1], (D,), jnp.float32), 0.25, 1.75)
    first_shift = scatter_about(streams_of[2], (D,), 0.5, 3.0, (), jnp.float32)
    input_weight = scatter_about(streams_of[3], (D, 3, HD), D ** -0.5, 0.15625, ((2, 8),))
    input_bias = draw_input_bias(jax.random.fold_in(streams_of[17], 71), 0)
    output_weight = scatter_about(streams_of[5], (HD, D), HD ** -0.5, 0.125, ((0, 8),))
    output_bias = scatter_about(streams_of[6], (D,), 0.5, 3.0, (), jnp.float32)
    second_gain = jnp.clip(1.0 + 0.15 * jax.random.normal(streams_of[7], (D,), jnp.float32), 0.25, 1.75)
    second_shift = scatter_about(streams_of[8], (D,), 0.5, 3.0, (), jnp.float32)
    expand_weight = scatter_about(streams_of[9], (D, FF), D ** -0.5, 0.15625, ((1, 8),))
    expand_bias = scatter_about(streams_of[10], (FF,), 0.5, 3.0, ((0, 8),), jnp.float32)
    contract_weight = scatter_about(streams_of[11], (FF, D), FF ** -0.5, 0.078125, ((0, 8),))
    contract_bias = scatter_about(streams_of[12], (D,), 0.5, 3.0, (), jnp.float32)
    key_cache = draw_key_cache(jax.random.fold_in(streams_of[17], 71), 0)
    value_cache = scatter_about(streams_of[14], (B, NS, HD), 1.0, 6.0, ((1, 32), (2, 8)))
    cache_fill = draw_cache_fill(jax.random.fold_in(streams_of[17], 71), 0)
    owner_shard = draw_owner_shard(jax.random.fold_in(streams_of[17], 71), 0)
    return dict(tokens=tokens, first_gain=first_gain, first_shift=first_shift, input_weight=input_weight, input_bias=input_bias, output_weight=output_weight, output_bias=output_bias, second_gain=second_gain, second_shift=second_shift, expand_weight=expand_weight, expand_bias=expand_bias, contract_weight=contract_weight, contract_bias=contract_bias, key_cache=key_cache, value_cache=value_cache, cache_fill=cache_fill, owner_shard=owner_shard)


def layer_norm(values, gain, shift):
    center = values - lax.optimization_barrier(jnp.mean(values, axis=-1, keepdims=True))
    spread = lax.optimization_barrier(jnp.mean(center * center, axis=-1, keepdims=True))
    return center * lax.rsqrt(spread + 1e-05) * gain + shift

def attend_request(item):
    query_row, key_rows, value_rows, usable_row = item
    scale = 1.0 / math.sqrt(HEAD_DIM)
    key_heads = key_rows.reshape(NS, HEADS, HEAD_DIM).astype(jnp.float32)
    value_heads = value_rows.reshape(NS, HEADS, HEAD_DIM).astype(jnp.float32)
    scores = jnp.einsum('hd,shd->hs', query_row, key_heads) * scale
    usable = usable_row[None, :]
    peaks = lax.optimization_barrier(jnp.max(jnp.where(usable, scores, -1e+30), axis=-1, keepdims=True))
    weights = jnp.where(usable, jnp.exp(scores - peaks), 0.0)
    totals = lax.optimization_barrier(jnp.sum(weights, axis=-1))
    blended = jnp.einsum('hs,shd->hd', weights.astype(jnp.bfloat16).astype(jnp.float32), value_heads)
    return (blended / totals[:, None]).reshape(HD)

def reference(tokens, first_gain, first_shift, input_weight, input_bias, output_weight, output_bias, second_gain, second_shift, expand_weight, expand_bias, contract_weight, contract_bias, key_cache, value_cache, cache_fill, owner_shard):
    live = cache_fill
    new_keys = key_cache
    new_values = value_cache
    request_ids = jnp.arange(B, dtype=jnp.int32)
    slot_ids = jnp.arange(NS, dtype=jnp.int32)
    slot_within = slot_ids % SEQ_DEV
    slot_shard = slot_ids // SEQ_DEV
    shard_ids = jnp.arange(NS // SEQ_DEV, dtype=jnp.int32)
    outputs = []
    for step_index in range(STEPS):
        rows = tokens[step_index].astype(jnp.float32)
        normed = layer_norm(rows, first_gain, first_shift).astype(jnp.bfloat16)
        packed = (jnp.einsum('rd,dch->rch', normed.astype(jnp.float32), input_weight.astype(jnp.float32)) + input_bias).astype(jnp.bfloat16)
        owners = owner_shard[step_index].astype(jnp.int32)
        target = jnp.take_along_axis(live, owners[:, None], axis=1)[:, 0]
        places = (owners * SEQ_DEV + target).astype(jnp.int32)
        new_keys = new_keys.at[request_ids, places].set(packed[:, 1])
        new_values = new_values.at[request_ids, places].set(packed[:, 2])
        live = live + (shard_ids[None, :] == owners[:, None]).astype(jnp.int32)
        limit = jnp.take(live, slot_shard, axis=1)
        usable = slot_within[None, :] < limit
        query_heads = packed[:, 0].reshape(B, HEADS, HEAD_DIM).astype(jnp.float32)
        attended = lax.map(attend_request, (query_heads, new_keys, new_values, usable)).astype(jnp.bfloat16)
        middle = rows + jnp.dot(attended, output_weight, preferred_element_type=jnp.float32) + output_bias
        second = layer_norm(middle, second_gain, second_shift).astype(jnp.bfloat16)
        hidden = jax.nn.gelu(jnp.dot(second, expand_weight, preferred_element_type=jnp.float32) + expand_bias, approximate=True).astype(jnp.bfloat16)
        result = jnp.dot(hidden, contract_weight, preferred_element_type=jnp.float32) + contract_bias + middle
        outputs.append(result.astype(jnp.bfloat16))
    return (jnp.stack(outputs), new_keys, new_values)
```

```python
import functools
import math

import jax
import jax.numpy as jnp
from jax import lax
from jax.experimental import pallas as pl
from jax.experimental.pallas import tpu as pltpu
from jax.sharding import PartitionSpec as P

HEAD_DIM = 64
MESH = pl.DeviceIdType.MESH
NEG = -1e30
F32 = jnp.float32
BF16 = jnp.bfloat16


def layer_norm(values, gain, shift):
    center = values - jnp.mean(values, axis=-1, keepdims=True)
    spread = jnp.mean(center * center, axis=-1, keepdims=True)
    return center * lax.rsqrt(spread + 1e-05) * gain + shift


def as_row(ref):
    return ref[...].reshape(1, ref.shape[0])


def dot_nt(a, b):
    return lax.dot_general(a, b, (((1,), (1,)), ((), ())), preferred_element_type=F32)


def layer_kernel(
    cfg,
    tok_h,
    g1_h,
    s1_h,
    win_h,
    bin_h,
    wout_h,
    bout_h,
    g2_h,
    s2_h,
    wexp_h,
    bexp_h,
    wcon_h,
    bcon_h,
    key_h,
    val_h,
    fill_h,
    own_h,
    hid_o,
    nk_o,
    nv_o,
    tok_v,
    g1_v,
    s1_v,
    win_v,
    bin_v,
    wout_v,
    bout_v,
    g2_v,
    s2_v,
    wexp_v,
    bexp_v,
    wcon_v,
    bcon_v,
    key_v,
    val_v,
    fill_s,
    own_s,
    x_v,
    kn_v,
    vn_v,
    mid_v,
    sbuf,
    rbuf,
    p2buf,
    r2buf,
    p3buf,
    r3buf,
    fbuf,
    obuf,
    load_sem,
    store_sem,
    send_sem,
    recv_sem,
):
    side, planes, steps, requests, slots, width, model, units = cfg
    chips = side * side
    shards = 2 * chips
    rows = steps * requests
    heads = width // HEAD_DIM
    cut_d = (model // 2) // 128 * 128
    win_d = model - cut_d
    pad_d = -(-win_d // 128) * 128
    cut_f = (units // 2) // 128 * 128
    win_f = units - cut_f

    shard = lax.axis_index("seq")
    z = lax.axis_index("tensor")
    chip = shard // 2
    core = shard % 2
    cx = chip // side
    cy = chip % side

    load_count = [0]

    def load(src, dst):
        copy = pltpu.make_async_copy(src, dst, load_sem.at[load_count[0]])
        load_count[0] += 1
        copy.start()
        return copy

    c_small = [load(tok_h, tok_v), load(g1_h, g1_v), load(s1_h, s1_v)]
    c_win = [load(win_h.at[0], win_v.at[0])]
    c_bin = load(bin_h, bin_v)
    c_fill = [load(fill_h, fill_s), load(own_h, own_s)]
    c_win += [load(win_h.at[1], win_v.at[1])]
    c_key = [load(key_h.at[b], key_v.at[b]) for b in range(requests)]
    c_win += [load(win_h.at[2], win_v.at[2])]
    c_val = [load(val_h.at[b], val_v.at[b]) for b in range(requests)]
    c_late = [load(bout_h, bout_v), load(g2_h, g2_v), load(s2_h, s2_v)]
    c_late += [load(bexp_h, bexp_v), load(bcon_h, bcon_v)]
    row_d = pl.multiple_of(core * cut_d, 128)
    row_f = pl.multiple_of(core * cut_f, 128)
    c_wout = load(wout_h.at[pl.ds(row_d, win_d)], wout_v)
    c_wexp = load(wexp_h.at[pl.ds(row_f, win_f)], wexp_v)
    c_wcon = load(wcon_h.at[pl.ds(row_f, win_f)], wcon_v)

    offsets = sorted(
        ((dx, dy) for dx in range(side) for dy in range(side)),
        key=lambda o: -(min(o[0], side - o[0]) + min(o[1], side - o[1])),
    )
    plane_peers = []
    for dx, dy in offsets:
        other = lax.rem(cx + dx, side) * side + lax.rem(cy + dy, side)
        if dx == 0 and dy == 0:
            plane_peers.append((other, 1 - core))
        else:
            plane_peers.append((other, 0))
            plane_peers.append((other, 1))
    z_offsets = sorted(range(planes), key=lambda d: -min(d, planes - d))
    column_peers = []
    for dz in z_offsets:
        other = lax.rem(z + dz, planes)
        if dz == 0:
            column_peers.append((other, None))
        else:
            column_peers.append((other, 0))
            column_peers.append((other, 1))

    barrier = pltpu.get_barrier_semaphore()
    signals = 0
    for other, k in plane_peers:
        pl.semaphore_signal(barrier, inc=1, device_id=(other * 2 + k, z), device_id_type=MESH)
        signals += 1
    for other, k in column_peers:
        if k is not None:
            pl.semaphore_signal(
                barrier, inc=1, device_id=(chip * 2 + k, other), device_id_type=MESH
            )
            signals += 1

    for c in c_small:
        c.wait()
    for t in range(steps):
        x_v[pl.ds(t * requests, requests), :] = tok_v[t].astype(F32)
    normed = layer_norm(x_v[...], as_row(g1_v), as_row(s1_v)).astype(BF16)
    c_bin.wait()
    packed = []
    for part in range(3):
        c_win[part].wait()
        packed.append(
            (
                jnp.dot(normed, win_v[part], preferred_element_type=F32)
                + bin_v[part : part + 1, :]
            ).astype(BF16)
        )
    query, key_new, value_new = packed
    kn_v[...] = key_new.astype(F32)
    vn_v[...] = value_new.astype(F32)

    for c in c_fill:
        c.wait()
    fills = [fill_s[b, shard] for b in range(requests)]
    owned = [[(own_s[t, b] == shard).astype(jnp.int32) for b in range(requests)] for t in range(steps)]
    places = []
    for b in range(requests):
        at = fills[b]
        row = []
        for t in range(steps):
            row.append(jnp.where(owned[t][b] > 0, at, -1))
            at = at + owned[t][b]
        places.append(row)

    total_rows = heads * rows
    row_id = lax.broadcasted_iota(jnp.int32, (total_rows, 1), 0)
    row_b = row_id % requests
    row_t = (row_id // requests) % steps
    fill_col = jnp.zeros((total_rows, 1), jnp.int32)
    for b in range(requests):
        fill_col = jnp.where(row_b == b, fills[b], fill_col)
    col = lax.broadcasted_iota(jnp.int32, (1, rows), 1)
    own_row = jnp.zeros((1, rows), jnp.int32)
    for t in range(steps):
        for b in range(requests):
            own_row = jnp.where(col == t * requests + b, owned[t][b], own_row)
    new_ok = (
        (col % requests == row_b) & (col // requests <= row_t) & (own_row > 0)
    )

    lane_head = lax.broadcasted_iota(jnp.int32, (rows, width), 1) // HEAD_DIM
    query_f = query.astype(F32)
    query_heads = jnp.concatenate(
        [jnp.where(lane_head == h, query_f, 0.0) for h in range(heads)], axis=0
    ).astype(BF16)
    scale = 1.0 / math.sqrt(HEAD_DIM)
    scores_new = jnp.where(new_ok, dot_nt(query_heads, key_new) * scale, NEG)
    scores = None
    for b in range(requests):
        c_key[b].wait()
        part = dot_nt(query_heads, key_v[b])
        scores = part if scores is None else jnp.where(row_b == b, part, scores)
    slot = lax.broadcasted_iota(jnp.int32, (total_rows, slots), 1)
    usable = slot < fill_col
    scores = jnp.where(usable, scores * scale, NEG)
    peaks = jnp.maximum(
        jnp.max(scores, axis=-1, keepdims=True), jnp.max(scores_new, axis=-1, keepdims=True)
    )
    weights = jnp.where(usable, jnp.exp(scores - peaks), 0.0)
    weights_new = jnp.where(new_ok, jnp.exp(scores_new - peaks), 0.0)
    totals = jnp.sum(weights, axis=-1, keepdims=True) + jnp.sum(
        weights_new, axis=-1, keepdims=True
    )
    blended = jnp.dot(weights_new.astype(BF16), value_new, preferred_element_type=F32)
    for b in range(requests):
        c_val[b].wait()
        blended = blended + jnp.dot(
            jnp.where(row_b == b, weights, 0.0).astype(BF16),
            val_v[b],
            preferred_element_type=F32,
        )
    lane = lax.broadcasted_iota(jnp.int32, (rows, 128), 1)
    merged = jnp.zeros((rows, width), F32)
    stats = jnp.zeros((rows, 128), F32)
    for h in range(heads):
        block = slice(h * rows, (h + 1) * rows)
        merged = jnp.where(lane_head == h, blended[block], merged)
        stats = jnp.where(lane == h, peaks[block], stats)
        stats = jnp.where(lane == heads + h, totals[block], stats)
    sbuf[:, 0, 0:width] = merged
    sbuf[:, 0, width : width + 128] = stats

    pl.semaphore_wait(barrier, signals)
    for other, k in plane_peers:
        pltpu.make_async_remote_copy(
            src_ref=sbuf.at[other],
            dst_ref=rbuf.at[shard],
            send_sem=send_sem.at[0],
            recv_sem=recv_sem.at[0],
            device_id=(other * 2 + k, z),
            device_id_type=MESH,
        ).start()
    rbuf[shard] = sbuf[chip]

    stores = []
    chunk = min(64, slots)
    for b in range(requests):

        def update(i, carry, b=b):
            start = pl.multiple_of(i * chunk, chunk)
            slot_id = start + lax.broadcasted_iota(jnp.int32, (chunk, 1), 0)
            for new, cache in ((kn_v, key_v), (vn_v, val_v)):
                block = cache[b, pl.ds(start, chunk), :].astype(F32)
                for t in range(steps):
                    r = t * requests + b
                    block = jnp.where(slot_id == places[b][t], new[r : r + 1, :], block)
                cache[b, pl.ds(start, chunk), :] = block.astype(BF16)
            return carry

        lax.fori_loop(0, slots // chunk, update, 0)
        for i, (cache, out) in enumerate(((key_v, nk_o), (val_v, nv_o))):
            copy = pltpu.make_async_copy(cache.at[b], out.at[b], store_sem.at[2 * b + i])
            copy.start()
            stores.append(copy)

    for c in c_late:
        c.wait()
    c_wout.wait()

    def wait_all(buf, count, sem):
        pltpu.make_async_copy(buf.at[pl.ds(0, count)], buf.at[pl.ds(0, count)], sem).wait()

    wait_all(rbuf, shards - 1, recv_sem.at[0])
    got = rbuf[:, 0, :]
    got_stats = got[:, width : width + 128]
    highest = jnp.max(got_stats, axis=0, keepdims=True)
    factor = jnp.exp(got_stats - highest)
    factor_at = pltpu.roll(factor, heads, 1)
    sums = jnp.sum(factor_at * got_stats, axis=0, keepdims=True)
    wide_head = lax.broadcasted_iota(jnp.int32, (shards, width), 1) // HEAD_DIM
    row_head = lax.broadcasted_iota(jnp.int32, (1, width), 1) // HEAD_DIM
    wide = jnp.zeros((shards, width), F32)
    below = jnp.ones((1, width), F32)
    for h in range(heads):
        wide = jnp.where(wide_head == h, factor[:, h : h + 1], wide)
        below = jnp.where(row_head == h, sums[:, heads + h : heads + h + 1], below)
    attended = jnp.sum(got[:, 0:width] * wide, axis=0, keepdims=True) / below
    attended = jnp.broadcast_to(attended, (16, width)).astype(BF16)

    slot_z = core * planes + z
    part = dot_nt(attended, wout_v[...])[0:1, :]
    part = jnp.concatenate([part, jnp.zeros((1, pad_d - win_d), F32)], axis=1)
    p2buf[0] = part
    r2buf[slot_z] = part
    for other, k in column_peers:
        pltpu.make_async_remote_copy(
            src_ref=p2buf.at[0],
            dst_ref=r2buf.at[slot_z],
            send_sem=send_sem.at[1],
            recv_sem=recv_sem.at[1],
            device_id=(chip * 2 + (1 - core if k is None else k), other),
            device_id_type=MESH,
        ).start()
    row_x = x_v[pl.ds(chip, 1), :] + as_row(bout_v)
    c_wexp.wait()
    c_wcon.wait()
    wait_all(r2buf, 2 * planes - 1, recv_sem.at[1])
    low = jnp.sum(r2buf[0:planes, 0, :], axis=0, keepdims=True)
    high = jnp.sum(r2buf[planes : 2 * planes, 0, :], axis=0, keepdims=True)
    middle = row_x + jnp.concatenate([low[:, :cut_d], high[:, :win_d]], axis=1)
    mid_v[:, 0:model] = middle + as_row(bcon_v)
    mid_v[:, model:] = jnp.zeros((1, mid_v.shape[1] - model), F32)

    second = layer_norm(middle, as_row(g2_v), as_row(s2_v))
    second = jnp.broadcast_to(second, (16, model)).astype(BF16)
    bias = as_row(bexp_v)
    bias = jnp.where(core == 0, bias[:, 0:win_f], bias[:, cut_f:units])
    hidden = jax.nn.gelu(dot_nt(second, wexp_v[...]) + bias, approximate=True)
    unit = lax.broadcasted_iota(jnp.int32, (16, win_f), 1)
    hidden = jnp.where(unit < jnp.where(core == 0, cut_f, win_f), hidden, 0.0).astype(BF16)
    part = jnp.dot(hidden, wcon_v[...], preferred_element_type=F32)[0:1, :]
    p3buf[:, 0:model] = part
    p3buf[:, model:] = jnp.zeros((1, p3buf.shape[1] - model), F32)

    for other, k in column_peers:
        to = 1 - core if k is None else k
        lanes = pl.ds(pl.multiple_of(to * cut_d, 128), pad_d)
        pltpu.make_async_remote_copy(
            src_ref=p3buf.at[:, lanes],
            dst_ref=r3buf.at[slot_z],
            send_sem=send_sem.at[2],
            recv_sem=recv_sem.at[2],
            device_id=(chip * 2 + to, other),
            device_id_type=MESH,
        ).start()
    own_lanes = pl.ds(row_d, pad_d)
    r3buf[slot_z] = p3buf[:, own_lanes]
    wait_all(r3buf, 2 * planes - 1, recv_sem.at[2])
    result = jnp.sum(r3buf[:, 0, :], axis=0, keepdims=True) + mid_v[:, own_lanes]
    slot_o = core * chips + chip
    fbuf[0] = result
    obuf[slot_o] = result

    for other, k in plane_peers:
        pltpu.make_async_remote_copy(
            src_ref=fbuf.at[0],
            dst_ref=obuf.at[slot_o],
            send_sem=send_sem.at[3],
            recv_sem=recv_sem.at[3],
            device_id=(other * 2 + k, z),
            device_id_type=MESH,
        ).start()
    for c in stores:
        c.wait()
    wait_all(rbuf, shards - 1, send_sem.at[0])
    wait_all(r2buf, 2 * planes - 1, send_sem.at[1])
    wait_all(r3buf, 2 * planes - 1, send_sem.at[2])
    wait_all(obuf, shards - 1, recv_sem.at[3])
    hid_o[:, 0:cut_d] = obuf[0:chips, 0, 0:cut_d].astype(BF16)
    hid_o[:, cut_d:model] = obuf[chips : 2 * chips, 0, 0:win_d].astype(BF16)
    wait_all(obuf, shards - 1, send_sem.at[3])


def per_device(
    side,
    planes,
    tokens,
    first_gain,
    first_shift,
    input_weight,
    input_bias,
    output_weight,
    output_bias,
    second_gain,
    second_shift,
    expand_weight,
    expand_bias,
    contract_weight,
    contract_bias,
    key_cache,
    value_cache,
    cache_fill,
    owner_shard,
):
    steps, requests, model = tokens.shape
    width = input_weight.shape[2]
    units = expand_weight.shape[1]
    slots = key_cache.shape[1]
    rows = steps * requests
    chips = side * side
    shards = 2 * chips
    cut_d = (model // 2) // 128 * 128
    win_d = model - cut_d
    pad_d = -(-win_d // 128) * 128
    win_f = units - (units // 2) // 128 * 128
    cfg = (side, planes, steps, requests, slots, width, model, units)
    args = (
        tokens,
        first_gain,
        first_shift,
        input_weight.transpose(1, 0, 2),
        input_bias,
        output_weight.T,
        output_bias,
        second_gain,
        second_shift,
        expand_weight.T,
        expand_bias,
        contract_weight,
        contract_bias,
        key_cache,
        value_cache,
        cache_fill,
        owner_shard,
    )
    row = pltpu.VMEM((model,), F32)
    hidden, new_keys, new_values = pl.pallas_call(
        functools.partial(layer_kernel, cfg),
        out_shape=(
            jax.ShapeDtypeStruct((rows, model), BF16),
            jax.ShapeDtypeStruct(key_cache.shape, BF16),
            jax.ShapeDtypeStruct(value_cache.shape, BF16),
        ),
        in_specs=[pl.BlockSpec(memory_space=pl.ANY)] * len(args),
        out_specs=(
            pl.BlockSpec(memory_space=pltpu.VMEM),
            pl.BlockSpec(memory_space=pl.ANY),
            pl.BlockSpec(memory_space=pl.ANY),
        ),
        scratch_shapes=[
            pltpu.VMEM(tokens.shape, BF16),
            row,
            row,
            pltpu.VMEM((3, model, width), BF16),
            pltpu.VMEM((3, width), F32),
            pltpu.VMEM((win_d, width), BF16),
            row,
            row,
            row,
            pltpu.VMEM((win_f, model), BF16),
            pltpu.VMEM((units,), F32),
            pltpu.VMEM((win_f, model), BF16),
            row,
            pltpu.VMEM(key_cache.shape, BF16),
            pltpu.VMEM(value_cache.shape, BF16),
            pltpu.SMEM(cache_fill.shape, jnp.int32),
            pltpu.SMEM(owner_shard.shape, jnp.int32),
            pltpu.VMEM((rows, model), F32),
            pltpu.VMEM((rows, width), F32),
            pltpu.VMEM((rows, width), F32),
            pltpu.VMEM((1, cut_d + pad_d), F32),
            pltpu.VMEM((rows, 1, width + 128), F32),
            pltpu.VMEM((shards, 1, width + 128), F32),
            pltpu.VMEM((1, 1, pad_d), F32),
            pltpu.VMEM((2 * planes, 1, pad_d), F32),
            pltpu.VMEM((1, cut_d + pad_d), F32),
            pltpu.VMEM((2 * planes, 1, pad_d), F32),
            pltpu.VMEM((1, 1, pad_d), F32),
            pltpu.VMEM((shards, 1, pad_d), F32),
            pltpu.SemaphoreType.DMA((17 + 2 + 2 * (requests - 1),)),
            pltpu.SemaphoreType.DMA((2 * requests,)),
            pltpu.SemaphoreType.DMA((4,)),
            pltpu.SemaphoreType.DMA((4,)),
        ],
        compiler_params=pltpu.CompilerParams(collective_id=0, has_side_effects=True),
        name="layer",
    )(*args)
    return (hidden.reshape(steps, requests, model), new_keys, new_values)


def solution(mesh):
    side = math.isqrt(mesh.shape["seq"] // 2)
    return jax.shard_map(
        functools.partial(per_device, side, mesh.shape["tensor"]),
        mesh=mesh,
        in_specs=(
            P(),
            P(),
            P(),
            P(None, None, "tensor"),
            P(None, "tensor"),
            P("tensor", None),
            P(),
            P(),
            P(),
            P(None, "tensor"),
            P("tensor"),
            P("tensor", None),
            P(),
            P(None, "seq", "tensor"),
            P(None, "seq", "tensor"),
            P(),
            P(),
        ),
        out_specs=(P(), P(None, "seq", "tensor"), P(None, "seq", "tensor")),
        check_vma=False,
    )
```

```python
import contextlib
import functools
import math

import jax
import jax.numpy as jnp
from jax import lax
from jax.experimental import pallas as pl
from jax.experimental.pallas import tpu as pltpu
from jax.sharding import PartitionSpec as P

HEAD_DIM = 64
MESH = pl.DeviceIdType.MESH
NEG = -1e30
F32 = jnp.float32
BF16 = jnp.bfloat16


def layer_norm(values, gain, shift):
    center = values - jnp.mean(values, axis=-1, keepdims=True)
    spread = jnp.mean(center * center, axis=-1, keepdims=True)
    return center * lax.rsqrt(spread + 1e-05) * gain + shift


TRACE = False


def scope(name):
    return jax.named_scope(name) if TRACE else contextlib.nullcontext()


def as_row(ref):
    return ref[...].reshape(1, ref.shape[0])


def dot_nt(a, b):
    return lax.dot_general(a, b, (((1,), (1,)), ((), ())), preferred_element_type=F32)


def layer_kernel(
    cfg,
    tok_h,
    g1_h,
    s1_h,
    win_h,
    bin_h,
    wout_h,
    bout_h,
    g2_h,
    s2_h,
    wexp_h,
    bexp_h,
    wcon_h,
    bcon_h,
    key_h,
    val_h,
    fill_h,
    own_h,
    hid_o,
    key_v,
    val_v,
    tok_v,
    g1_v,
    s1_v,
    win_v,
    bin_v,
    wout_v,
    bout_v,
    g2_v,
    s2_v,
    wexp_v,
    bexp_v,
    wcon_v,
    bcon_v,
    fill_s,
    own_s,
    x_v,
    kn_v,
    vn_v,
    sbuf,
    rbuf,
    p2buf,
    r2buf,
    p3buf,
    r3buf,
    fbuf,
    obuf,
    load_sem,
    send_sem,
    recv_sem,
):
    side, planes, steps, requests, slots, width, model, units = cfg
    half = side // 2
    chips = side * side
    shards = 2 * chips
    rows = steps * requests
    heads = width // HEAD_DIM
    wide_d = p2buf.shape[-1]

    shard = lax.axis_index("seq")
    z = lax.axis_index("tensor")
    chip = shard // 2
    core = shard % 2
    cx = chip // side
    cy = chip % side

    def row_of(x, y, k):
        return 2 * (lax.rem(x, half) * side + lax.rem(y + half * (x // half), side)) + k

    my_row = row_of(cx, cy, core)

    load_count = [0]

    def load(src, dst):
        copy = pltpu.make_async_copy(src, dst, load_sem.at[load_count[0]])
        load_count[0] += 1
        copy.start()
        return copy

    with scope("issue"):
        c_small = [load(tok_h, tok_v), load(g1_h, g1_v), load(s1_h, s1_v)]
        c_win = [load(win_h.at[0], win_v.at[0])]
        c_bin = load(bin_h, bin_v)
        c_fill = [load(fill_h, fill_s), load(own_h, own_s)]
        c_key = [load(key_h.at[b], key_v.at[b]) for b in range(requests)]
        c_win += [load(win_h.at[1], win_v.at[1]), load(win_h.at[2], win_v.at[2])]
        c_val = [load(val_h.at[b], val_v.at[b]) for b in range(requests)]

    def distance(o):
        return min(o[0], side - o[0]) + min(o[1], side - o[1])

    offsets = sorted(
        ((dx, dy) for dx in range(side) for dy in range(side)), key=lambda o: -distance(o)
    )
    plane_peers = []
    for dx, dy in offsets:
        other = (lax.rem(cx + dx, side), lax.rem(cy + dy, side))
        if dx == 0 and dy == 0:
            plane_peers.append((*other, 1 - core))
        else:
            plane_peers.append((*other, 0))
            plane_peers.append((*other, 1))
    column_peers = [
        lax.rem(z + dz, planes)
        for dz in sorted(range(1, planes), key=lambda d: -min(d, planes - d))
    ]

    def seq_of(x, y, k):
        return (x * side + y) * 2 + k

    barrier = pltpu.get_barrier_semaphore()
    with scope("signals"):
        for peer in plane_peers:
            pl.semaphore_signal(
                barrier, inc=1, device_id=(seq_of(*peer), z), device_id_type=MESH
            )
        for other in column_peers:
            pl.semaphore_signal(barrier, inc=1, device_id=(shard, other), device_id_type=MESH)

    with scope("norm1"):
        for c in c_small:
            c.wait()
        for t in range(steps):
            x_v[pl.ds(t * requests, requests), :] = tok_v[t].astype(F32)
        normed = layer_norm(x_v[...], as_row(g1_v), as_row(s1_v)).astype(BF16)
        c_bin.wait()

    def project(part):
        c_win[part].wait()
        return (
            jnp.dot(normed, win_v[part], preferred_element_type=F32) + bin_v[part : part + 1, :]
        ).astype(BF16)

    with scope("query"):
        query = project(0)

    for c in c_fill:
        c.wait()
    fills = [fill_s[b, shard] for b in range(requests)]
    owned = [
        [(own_s[t, b] == shard).astype(jnp.int32) for b in range(requests)] for t in range(steps)
    ]
    places = []
    for b in range(requests):
        at = fills[b]
        row = []
        for t in range(steps):
            row.append(jnp.where(owned[t][b] > 0, at, -1))
            at = at + owned[t][b]
        places.append(row)

    total_rows = heads * rows
    row_id = lax.broadcasted_iota(jnp.int32, (total_rows, 1), 0)
    row_b = row_id % requests
    row_t = (row_id // requests) % steps
    fill_col = jnp.zeros((total_rows, 1), jnp.int32)
    for b in range(requests):
        fill_col = jnp.where(row_b == b, fills[b], fill_col)
    col = lax.broadcasted_iota(jnp.int32, (1, rows), 1)
    own_row = jnp.zeros((1, rows), jnp.int32)
    for t in range(steps):
        for b in range(requests):
            own_row = jnp.where(col == t * requests + b, owned[t][b], own_row)
    new_ok = (col % requests == row_b) & (col // requests <= row_t) & (own_row > 0)

    lane_head = lax.broadcasted_iota(jnp.int32, (rows, width), 1) // HEAD_DIM
    query_f = query.astype(F32)
    query_heads = jnp.concatenate(
        [jnp.where(lane_head == h, query_f, 0.0) for h in range(heads)], axis=0
    ).astype(BF16)
    scale = 1.0 / math.sqrt(HEAD_DIM)
    scores = None
    with scope("scores"):
        for b in range(requests):
            c_key[b].wait()
            part = dot_nt(query_heads, key_v[b])
            scores = part if scores is None else jnp.where(row_b == b, part, scores)
    with scope("keyvalue"):
        key_new = project(1)
        value_new = project(2)
        kn_v[...] = key_new.astype(F32)
        vn_v[...] = value_new.astype(F32)
    with scope("attend"):
        scores_new = jnp.where(new_ok, dot_nt(query_heads, key_new) * scale, NEG)
        slot = lax.broadcasted_iota(jnp.int32, (total_rows, slots), 1)
        usable = slot < fill_col
        scores = jnp.where(usable, scores * scale, NEG)
        peaks = jnp.maximum(
            jnp.max(scores, axis=-1, keepdims=True), jnp.max(scores_new, axis=-1, keepdims=True)
        )
        weights = jnp.where(usable, jnp.exp(scores - peaks), 0.0)
        weights_new = jnp.where(new_ok, jnp.exp(scores_new - peaks), 0.0)
        totals = jnp.sum(weights, axis=-1, keepdims=True) + jnp.sum(
            weights_new, axis=-1, keepdims=True
        )
        blended = jnp.dot(weights_new.astype(BF16), value_new, preferred_element_type=F32)
        for b in range(requests):
            c_val[b].wait()
            blended = blended + jnp.dot(
                jnp.where(row_b == b, weights, 0.0).astype(BF16),
                val_v[b],
                preferred_element_type=F32,
            )
        lane = lax.broadcasted_iota(jnp.int32, (rows, 128), 1)
        merged = jnp.zeros((rows, width), F32)
        stats = jnp.zeros((rows, 128), F32)
        for h in range(heads):
            block = slice(h * rows, (h + 1) * rows)
            merged = jnp.where(lane_head == h, blended[block], merged)
            stats = jnp.where(lane == h, peaks[block], stats)
            stats = jnp.where(lane == heads + h, totals[block], stats)
        sbuf[:, 0, 0:width] = merged
        sbuf[:, 0, width : width + 128] = stats

    with scope("barrier"):
        pl.semaphore_wait(barrier, len(plane_peers) + len(column_peers))
    with scope("send1"):
        for peer in plane_peers:
            pltpu.make_async_remote_copy(
                src_ref=sbuf.at[row_of(*peer)],
                dst_ref=rbuf.at[shard],
                send_sem=send_sem.at[0],
                recv_sem=recv_sem.at[0],
                device_id=(seq_of(*peer), z),
                device_id_type=MESH,
            ).start()
        rbuf[shard] = sbuf[my_row]
        c_wout = load(wout_h, wout_v)
        c_late = [load(bout_h, bout_v), load(g2_h, g2_v), load(s2_h, s2_v)]
        c_late += [load(bexp_h, bexp_v), load(bcon_h, bcon_v)]
        c_wexp = load(wexp_h, wexp_v)
        c_wcon = load(wcon_h, wcon_v)

    with scope("caches"):
        chunk = min(64, slots)
        for b in range(requests):

            def update(i, carry, b=b):
                start = pl.multiple_of(i * chunk, chunk)
                slot_id = start + lax.broadcasted_iota(jnp.int32, (chunk, 1), 0)
                for new, cache in ((kn_v, key_v), (vn_v, val_v)):
                    block = cache[b, pl.ds(start, chunk), :].astype(F32)
                    for t in range(steps):
                        r = t * requests + b
                        block = jnp.where(slot_id == places[b][t], new[r : r + 1, :], block)
                    cache[b, pl.ds(start, chunk), :] = block.astype(BF16)
                return carry

            lax.fori_loop(0, slots // chunk, update, 0)

    with scope("wlate"):
        for c in c_late:
            c.wait()
        c_wout.wait()

    def wait_all(buf, count, sem):
        pltpu.make_async_copy(buf.at[pl.ds(0, count)], buf.at[pl.ds(0, count)], sem).wait()

    with scope("wait1"):
        wait_all(rbuf, shards - 1, recv_sem.at[0])
    with scope("project"):
        got = rbuf[:, 0, :]
        got_stats = got[:, width : width + 128]
        highest = jnp.max(got_stats, axis=0, keepdims=True)
        factor = jnp.exp(got_stats - highest)
        factor_at = pltpu.roll(factor, heads, 1)
        sums = jnp.sum(factor_at * got_stats, axis=0, keepdims=True)
        wide_head = lax.broadcasted_iota(jnp.int32, (shards, width), 1) // HEAD_DIM
        row_head = lax.broadcasted_iota(jnp.int32, (1, width), 1) // HEAD_DIM
        wide = jnp.zeros((shards, width), F32)
        below = jnp.ones((1, width), F32)
        for h in range(heads):
            wide = jnp.where(wide_head == h, factor[:, h : h + 1], wide)
            below = jnp.where(row_head == h, sums[:, heads + h : heads + h + 1], below)
        attended = jnp.sum(got[:, 0:width] * wide, axis=0, keepdims=True) / below
        attended = jnp.broadcast_to(attended, (16, width)).astype(BF16)
        part = dot_nt(attended, wout_v[...])[0:1, :]
        part = jnp.concatenate([part, jnp.zeros((1, wide_d - model), F32)], axis=1)

    def exchange(part, out, into, n):
        out[0] = part
        into[z] = part
        for other in column_peers:
            pltpu.make_async_remote_copy(
                src_ref=out.at[0],
                dst_ref=into.at[z],
                send_sem=send_sem.at[n],
                recv_sem=recv_sem.at[n],
                device_id=(shard, other),
                device_id_type=MESH,
            ).start()

    def collect(into, n):
        wait_all(into, planes - 1, recv_sem.at[n])
        return jnp.sum(into[:, 0, :], axis=0, keepdims=True)

    with scope("send2"):
        exchange(part, p2buf, r2buf, 1)
        row_x = x_v[pl.ds(my_row, 1), :] + as_row(bout_v)
        c_wexp.wait()
        c_wcon.wait()
    with scope("wait2"):
        heads_sum = collect(r2buf, 1)
    with scope("ffn"):
        middle = row_x + heads_sum[:, 0:model]
        second = layer_norm(middle, as_row(g2_v), as_row(s2_v))
        second = jnp.broadcast_to(second, (16, model)).astype(BF16)
        hidden = jax.nn.gelu(dot_nt(second, wexp_v[...]) + as_row(bexp_v), approximate=True)
        part = jnp.dot(hidden.astype(BF16), wcon_v[...], preferred_element_type=F32)[0:1, :]
        part = jnp.concatenate([part, jnp.zeros((1, wide_d - model), F32)], axis=1)
    with scope("send3"):
        exchange(part, p3buf, r3buf, 2)
        rest = jnp.concatenate(
            [middle + as_row(bcon_v), jnp.zeros((1, wide_d - model), F32)], axis=1
        )
    with scope("wait3"):
        units_sum = collect(r3buf, 2)

    with scope("send4"):
        result = units_sum + rest
        fbuf[0] = result
        obuf[my_row] = result
        near = []
        for o in offsets:
            opposite = ((o[0] + half) % side, (o[1] + half) % side)
            if (distance(o), o) < (distance(opposite), opposite):
                near.append(o)
        for dx, dy in near:
            other = (lax.rem(cx + dx, side), lax.rem(cy + dy, side))
            for k in (1 - core,) if (dx, dy) == (0, 0) else (0, 1):
                pltpu.make_async_remote_copy(
                    src_ref=fbuf.at[0],
                    dst_ref=obuf.at[my_row],
                    send_sem=send_sem.at[3],
                    recv_sem=recv_sem.at[3],
                    device_id=(seq_of(*other, k), z),
                    device_id_type=MESH,
                ).start()
        wait_all(rbuf, shards - 1, send_sem.at[0])
        wait_all(r2buf, planes - 1, send_sem.at[1])
        wait_all(r3buf, planes - 1, send_sem.at[2])
    with scope("wait4"):
        wait_all(obuf, rows - 1, recv_sem.at[3])
    with scope("finish"):
        for t in range(steps):
            hid_o[t] = obuf[t * requests : (t + 1) * requests, 0, 0:model].astype(BF16)
        wait_all(obuf, rows - 1, send_sem.at[3])


def write_kernel(hid_i, key_i, val_i, hid_o, key_o, val_o, sem):
    pairs = ((key_i, key_o), (val_i, val_o), (hid_i, hid_o))
    copies = [pltpu.make_async_copy(src, dst, sem.at[i]) for i, (src, dst) in enumerate(pairs)]
    for copy in copies:
        copy.start()
    for copy in copies:
        copy.wait()


def per_device(
    side,
    planes,
    tokens,
    first_gain,
    first_shift,
    input_weight,
    input_bias,
    output_weight,
    output_bias,
    second_gain,
    second_shift,
    expand_weight,
    expand_bias,
    contract_weight,
    contract_bias,
    key_cache,
    value_cache,
    cache_fill,
    owner_shard,
):
    steps, requests, model = tokens.shape
    width = input_weight.shape[2]
    units = expand_weight.shape[1]
    slots = key_cache.shape[1]
    rows = steps * requests
    shards = 2 * side * side
    wide_d = -(-model // 128) * 128
    cfg = (side, planes, steps, requests, slots, width, model, units)
    args = (
        tokens,
        first_gain,
        first_shift,
        input_weight.transpose(1, 0, 2),
        input_bias,
        output_weight.T,
        output_bias,
        second_gain,
        second_shift,
        expand_weight.T,
        expand_bias,
        contract_weight,
        contract_bias,
        key_cache,
        value_cache,
        cache_fill,
        owner_shard,
    )
    row = pltpu.VMEM((model,), F32)
    outs = (tokens.shape, key_cache.shape, value_cache.shape)
    results = pl.pallas_call(
        functools.partial(layer_kernel, cfg),
        out_shape=tuple(pltpu.VMEM(shape, BF16) for shape in outs),
        in_specs=[pl.BlockSpec(memory_space=pl.ANY)] * len(args),
        out_specs=tuple(pl.BlockSpec(memory_space=pltpu.VMEM) for _ in outs),
        scratch_shapes=[
            pltpu.VMEM(tokens.shape, BF16),
            row,
            row,
            pltpu.VMEM((3, model, width), BF16),
            pltpu.VMEM((3, width), F32),
            pltpu.VMEM((model, width), BF16),
            row,
            row,
            row,
            pltpu.VMEM((units, model), BF16),
            pltpu.VMEM((units,), F32),
            pltpu.VMEM((units, model), BF16),
            row,
            pltpu.SMEM(cache_fill.shape, jnp.int32),
            pltpu.SMEM(owner_shard.shape, jnp.int32),
            pltpu.VMEM((rows, model), F32),
            pltpu.VMEM((rows, width), F32),
            pltpu.VMEM((rows, width), F32),
            pltpu.VMEM((rows, 1, width + 128), F32),
            pltpu.VMEM((shards, 1, width + 128), F32),
            pltpu.VMEM((1, 1, wide_d), F32),
            pltpu.VMEM((planes, 1, wide_d), F32),
            pltpu.VMEM((1, 1, wide_d), F32),
            pltpu.VMEM((planes, 1, wide_d), F32),
            pltpu.VMEM((1, 1, wide_d), F32),
            pltpu.VMEM((rows, 1, wide_d), F32),
            pltpu.SemaphoreType.DMA((17 + 2 + 2 * (requests - 1),)),
            pltpu.SemaphoreType.DMA((4,)),
            pltpu.SemaphoreType.DMA((4,)),
        ],
        compiler_params=pltpu.CompilerParams(collective_id=0, has_side_effects=True),
        name="layer",
    )(*args)
    return pl.pallas_call(
        write_kernel,
        out_shape=tuple(jax.ShapeDtypeStruct(shape, BF16) for shape in outs),
        in_specs=[pl.BlockSpec(memory_space=pltpu.VMEM)] * len(outs),
        out_specs=tuple(pl.BlockSpec(memory_space=pl.ANY) for _ in outs),
        scratch_shapes=[pltpu.SemaphoreType.DMA((len(outs),))],
        name="write",
    )(*(pltpu.with_memory_space_constraint(r, pltpu.VMEM) for r in results))


def solution(mesh):
    side = math.isqrt(mesh.shape["seq"] // 2)
    return jax.shard_map(
        functools.partial(per_device, side, mesh.shape["tensor"]),
        mesh=mesh,
        in_specs=(
            P(),
            P(),
            P(),
            P(None, None, "tensor"),
            P(None, "tensor"),
            P("tensor", None),
            P(),
            P(),
            P(),
            P(None, "tensor"),
            P("tensor"),
            P("tensor", None),
            P(),
            P(None, "seq", "tensor"),
            P(None, "seq", "tensor"),
            P(),
            P(),
        ),
        out_specs=(P(), P(None, "seq", "tensor"), P(None, "seq", "tensor")),
        check_vma=False,
    )
```

```python
import contextlib
import functools
import math

import jax
import jax.numpy as jnp
from jax import lax
from jax.experimental import pallas as pl
from jax.experimental.pallas import tpu as pltpu
from jax.sharding import PartitionSpec as P

HEAD_DIM = 64
MESH = pl.DeviceIdType.MESH
NEG = -1e30
F32 = jnp.float32
BF16 = jnp.bfloat16


def layer_norm(values, gain, shift):
    center = values - jnp.mean(values, axis=-1, keepdims=True)
    spread = jnp.mean(center * center, axis=-1, keepdims=True)
    return center * lax.rsqrt(spread + 1e-05) * gain + shift


TRACE = False


def scope(name):
    return jax.named_scope(name) if TRACE else contextlib.nullcontext()


def as_row(ref):
    return ref[...].reshape(1, ref.shape[0])


def dot_nt(a, b):
    return lax.dot_general(a, b, (((1,), (1,)), ((), ())), preferred_element_type=F32)


def layer_kernel(
    cfg,
    tok_h,
    g1_h,
    s1_h,
    win_h,
    bin_h,
    wout_h,
    bout_h,
    g2_h,
    s2_h,
    wexp_h,
    bexp_h,
    wcon_h,
    bcon_h,
    key_h,
    val_h,
    fill_h,
    own_h,
    hid_o,
    key_v,
    val_v,
    tok_v,
    g1_v,
    s1_v,
    win_v,
    bin_v,
    wout_v,
    bout_v,
    g2_v,
    s2_v,
    wexp_v,
    bexp_v,
    wcon_v,
    bcon_v,
    fill_s,
    own_s,
    x_v,
    kn_v,
    vn_v,
    sbuf,
    rbuf,
    p2buf,
    r2buf,
    p3buf,
    r3buf,
    fbuf,
    obuf,
    load_sem,
    send_sem,
    recv_sem,
):
    side, planes, steps, requests, slots, width, model, units = cfg
    half = side // 2
    chips = side * side
    shards = 2 * chips
    rows = steps * requests
    heads = width // HEAD_DIM
    wide_d = p2buf.shape[-1]

    shard = lax.axis_index("seq")
    z = lax.axis_index("tensor")
    chip = shard // 2
    core = shard % 2
    cx = chip // side
    cy = chip % side

    def row_of(x, y, k):
        return 2 * (lax.rem(x, half) * side + lax.rem(y + half * (x // half), side)) + k

    my_row = row_of(cx, cy, core)

    load_count = [0]

    def load(src, dst):
        copy = pltpu.make_async_copy(src, dst, load_sem.at[load_count[0]])
        load_count[0] += 1
        copy.start()
        return copy

    with scope("issue"):
        c_small = [load(tok_h, tok_v), load(g1_h, g1_v), load(s1_h, s1_v)]
        c_win = load(win_h.at[0], win_v.at[0])
        c_bin = load(bin_h, bin_v)
        c_fill = [load(fill_h, fill_s), load(own_h, own_s)]
        c_key = load(key_h, key_v)
        c_rest = [load(win_h.at[pl.ds(1, 2)], win_v.at[pl.ds(1, 2)]), load(val_h, val_v)]

    def distance(o):
        return min(o[0], side - o[0]) + min(o[1], side - o[1])

    offsets = sorted(
        ((dx, dy) for dx in range(side) for dy in range(side)), key=lambda o: -distance(o)
    )
    plane_peers = []
    for dx, dy in offsets:
        other = (lax.rem(cx + dx, side), lax.rem(cy + dy, side))
        if dx == 0 and dy == 0:
            plane_peers.append((*other, 1 - core))
        else:
            plane_peers.append((*other, 0))
            plane_peers.append((*other, 1))
    column_steps = sorted(range(1, planes), key=lambda d: -min(d, planes - d))
    column_peers = [lax.rem(z + dz, planes) for dz in column_steps]

    def seq_of(x, y, k):
        return (x * side + y) * 2 + k

    barrier = pltpu.get_barrier_semaphore()
    with scope("signals"):
        hops = [distance(o) for o in offsets for _ in range(2)][: len(plane_peers)]
        greet = [(h, (seq_of(*peer), z)) for h, peer in zip(hops, plane_peers)]
        greet += [(min(dz, planes - dz), (shard, o)) for dz, o in zip(column_steps, column_peers)]
        for _, device in sorted(greet, key=lambda g: -g[0]):
            pl.semaphore_signal(barrier, inc=1, device_id=device, device_id_type=MESH)

    with scope("norm1"):
        for c in c_small:
            c.wait()
        for t in range(steps):
            x_v[pl.ds(t * requests, requests), :] = tok_v[t].astype(F32)
        normed = layer_norm(x_v[...], as_row(g1_v), as_row(s1_v)).astype(BF16)
        c_bin.wait()

    with scope("load1"):
        for c in (c_win, *c_fill, c_key):
            c.wait()

    def project(part):
        return (
            jnp.dot(normed, win_v[part], preferred_element_type=F32) + bin_v[part : part + 1, :]
        ).astype(BF16)

    with scope("query"):
        query = project(0)

    fills = [fill_s[b, shard] for b in range(requests)]
    owned = [
        [(own_s[t, b] == shard).astype(jnp.int32) for b in range(requests)] for t in range(steps)
    ]
    places = []
    for b in range(requests):
        at = fills[b]
        row = []
        for t in range(steps):
            row.append(jnp.where(owned[t][b] > 0, at, -1))
            at = at + owned[t][b]
        places.append(row)

    total_rows = heads * rows
    row_id = lax.broadcasted_iota(jnp.int32, (total_rows, 1), 0)
    row_b = row_id % requests
    row_t = (row_id // requests) % steps
    fill_col = jnp.zeros((total_rows, 1), jnp.int32)
    for b in range(requests):
        fill_col = jnp.where(row_b == b, fills[b], fill_col)
    col = lax.broadcasted_iota(jnp.int32, (1, rows), 1)
    own_row = jnp.zeros((1, rows), jnp.int32)
    for t in range(steps):
        for b in range(requests):
            own_row = jnp.where(col == t * requests + b, owned[t][b], own_row)
    new_ok = (col % requests == row_b) & (col // requests <= row_t) & (own_row > 0)

    lane_head = lax.broadcasted_iota(jnp.int32, (rows, width), 1) // HEAD_DIM
    query_f = query.astype(F32)
    query_heads = jnp.concatenate(
        [jnp.where(lane_head == h, query_f, 0.0) for h in range(heads)], axis=0
    ).astype(BF16)
    scale = 1.0 / math.sqrt(HEAD_DIM)
    scores = None
    with scope("scores"):
        for b in range(requests):
            part = dot_nt(query_heads, key_v[b])
            scores = part if scores is None else jnp.where(row_b == b, part, scores)
    with scope("load2"):
        for c in c_rest:
            c.wait()
    with scope("keyvalue"):
        key_new = project(1)
        value_new = project(2)
        kn_v[...] = key_new.astype(F32)
        vn_v[...] = value_new.astype(F32)
    with scope("attend"):
        scores_new = jnp.where(new_ok, dot_nt(query_heads, key_new) * scale, NEG)
        slot = lax.broadcasted_iota(jnp.int32, (total_rows, slots), 1)
        usable = slot < fill_col
        scores = jnp.where(usable, scores * scale, NEG)
        peaks = jnp.maximum(
            jnp.max(scores, axis=-1, keepdims=True), jnp.max(scores_new, axis=-1, keepdims=True)
        )
        weights = jnp.where(usable, jnp.exp(scores - peaks), 0.0)
        weights_new = jnp.where(new_ok, jnp.exp(scores_new - peaks), 0.0)
        totals = jnp.sum(weights, axis=-1, keepdims=True) + jnp.sum(
            weights_new, axis=-1, keepdims=True
        )
        blended = jnp.dot(weights_new.astype(BF16), value_new, preferred_element_type=F32)
        for b in range(requests):
            blended = blended + jnp.dot(
                jnp.where(row_b == b, weights, 0.0).astype(BF16),
                val_v[b],
                preferred_element_type=F32,
            )
        lane = lax.broadcasted_iota(jnp.int32, (rows, 128), 1)
        merged = jnp.zeros((rows, width), F32)
        stats = jnp.zeros((rows, 128), F32)
        for h in range(heads):
            block = slice(h * rows, (h + 1) * rows)
            merged = jnp.where(lane_head == h, blended[block], merged)
            stats = jnp.where(lane == h, peaks[block], stats)
            stats = jnp.where(lane == heads + h, totals[block], stats)
        sbuf[:, 0, 0:width] = merged
        sbuf[:, 0, width : width + 128] = stats

    with scope("barrier"):
        pl.semaphore_wait(barrier, len(plane_peers) + len(column_peers))
    with scope("send1"):
        for peer in plane_peers:
            pltpu.make_async_remote_copy(
                src_ref=sbuf.at[row_of(*peer)],
                dst_ref=rbuf.at[shard],
                send_sem=send_sem.at[0],
                recv_sem=recv_sem.at[0],
                device_id=(seq_of(*peer), z),
                device_id_type=MESH,
            ).start()
        rbuf[shard] = sbuf[my_row]
        c_wout = load(wout_h, wout_v)
        c_late = [load(bout_h, bout_v), load(g2_h, g2_v), load(s2_h, s2_v)]
        c_late += [load(bexp_h, bexp_v), load(bcon_h, bcon_v)]
        c_wexp = load(wexp_h, wexp_v)
        c_wcon = load(wcon_h, wcon_v)

    with scope("caches"):
        chunk = min(64, slots)
        for b in range(requests):

            def update(i, carry, b=b):
                start = pl.multiple_of(i * chunk, chunk)
                slot_id = start + lax.broadcasted_iota(jnp.int32, (chunk, 1), 0)
                for new, cache in ((kn_v, key_v), (vn_v, val_v)):
                    block = cache[b, pl.ds(start, chunk), :].astype(F32)
                    for t in range(steps):
                        r = t * requests + b
                        block = jnp.where(slot_id == places[b][t], new[r : r + 1, :], block)
                    cache[b, pl.ds(start, chunk), :] = block.astype(BF16)
                return carry

            lax.fori_loop(0, slots // chunk, update, 0)

    with scope("wlate"):
        for c in c_late:
            c.wait()
        c_wout.wait()

    def wait_all(buf, count, sem):
        pltpu.make_async_copy(buf.at[pl.ds(0, count)], buf.at[pl.ds(0, count)], sem).wait()

    with scope("wait1"):
        wait_all(rbuf, shards - 1, recv_sem.at[0])
    with scope("project"):
        got = rbuf[:, 0, :]
        got_stats = got[:, width : width + 128]
        highest = jnp.max(got_stats, axis=0, keepdims=True)
        factor = jnp.exp(got_stats - highest)
        factor_at = pltpu.roll(factor, heads, 1)
        sums = jnp.sum(factor_at * got_stats, axis=0, keepdims=True)
        wide_head = lax.broadcasted_iota(jnp.int32, (shards, width), 1) // HEAD_DIM
        row_head = lax.broadcasted_iota(jnp.int32, (1, width), 1) // HEAD_DIM
        wide = jnp.zeros((shards, width), F32)
        below = jnp.ones((1, width), F32)
        for h in range(heads):
            wide = jnp.where(wide_head == h, factor[:, h : h + 1], wide)
            below = jnp.where(row_head == h, sums[:, heads + h : heads + h + 1], below)
        attended = jnp.sum(got[:, 0:width] * wide, axis=0, keepdims=True) / below
        attended = jnp.broadcast_to(attended, (16, width)).astype(BF16)
        part = dot_nt(attended, wout_v[...])[0:1, :]
        part = jnp.concatenate([part, jnp.zeros((1, wide_d - model), F32)], axis=1)

    def exchange(part, out, into, n):
        out[0] = part
        into[z] = part
        for other in column_peers:
            pltpu.make_async_remote_copy(
                src_ref=out.at[0],
                dst_ref=into.at[z],
                send_sem=send_sem.at[n],
                recv_sem=recv_sem.at[n],
                device_id=(shard, other),
                device_id_type=MESH,
            ).start()

    def collect(into, n):
        wait_all(into, planes - 1, recv_sem.at[n])
        return jnp.sum(into[:, 0, :], axis=0, keepdims=True)

    with scope("send2"):
        exchange(part, p2buf, r2buf, 1)
        row_x = x_v[pl.ds(my_row, 1), :] + as_row(bout_v)
        c_wexp.wait()
        c_wcon.wait()
    with scope("wait2"):
        heads_sum = collect(r2buf, 1)
    with scope("ffn"):
        middle = row_x + heads_sum[:, 0:model]
        second = layer_norm(middle, as_row(g2_v), as_row(s2_v))
        second = jnp.broadcast_to(second, (16, model)).astype(BF16)
        hidden = jax.nn.gelu(dot_nt(second, wexp_v[...]) + as_row(bexp_v), approximate=True)
        part = jnp.dot(hidden.astype(BF16), wcon_v[...], preferred_element_type=F32)[0:1, :]
        part = jnp.concatenate([part, jnp.zeros((1, wide_d - model), F32)], axis=1)
    with scope("send3"):
        exchange(part, p3buf, r3buf, 2)
        rest = jnp.concatenate(
            [middle + as_row(bcon_v), jnp.zeros((1, wide_d - model), F32)], axis=1
        )
    with scope("wait3"):
        units_sum = collect(r3buf, 2)

    with scope("send4"):
        result = units_sum + rest
        fbuf[0] = result
        obuf[my_row] = result
        near = []
        for o in offsets:
            opposite = ((o[0] + half) % side, (o[1] + half) % side)
            if (distance(o), o) < (distance(opposite), opposite):
                near.append(o)
        for dx, dy in near:
            other = (lax.rem(cx + dx, side), lax.rem(cy + dy, side))
            for k in (1 - core,) if (dx, dy) == (0, 0) else (0, 1):
                pltpu.make_async_remote_copy(
                    src_ref=fbuf.at[0],
                    dst_ref=obuf.at[my_row],
                    send_sem=send_sem.at[3],
                    recv_sem=recv_sem.at[3],
                    device_id=(seq_of(*other, k), z),
                    device_id_type=MESH,
                ).start()
        wait_all(rbuf, shards - 1, send_sem.at[0])
        wait_all(r2buf, planes - 1, send_sem.at[1])
        wait_all(r3buf, planes - 1, send_sem.at[2])
    with scope("wait4"):
        wait_all(obuf, rows - 1, recv_sem.at[3])
    with scope("finish"):
        for t in range(steps):
            hid_o[t] = obuf[t * requests : (t + 1) * requests, 0, 0:model].astype(BF16)
        wait_all(obuf, rows - 1, send_sem.at[3])


def write_kernel(hid_i, key_i, val_i, hid_o, key_o, val_o, sem):
    pairs = ((key_i, key_o), (val_i, val_o), (hid_i, hid_o))
    copies = [pltpu.make_async_copy(src, dst, sem.at[i]) for i, (src, dst) in enumerate(pairs)]
    for copy in copies:
        copy.start()
    for copy in copies:
        copy.wait()


def per_device(
    side,
    planes,
    tokens,
    first_gain,
    first_shift,
    input_weight,
    input_bias,
    output_weight,
    output_bias,
    second_gain,
    second_shift,
    expand_weight,
    expand_bias,
    contract_weight,
    contract_bias,
    key_cache,
    value_cache,
    cache_fill,
    owner_shard,
):
    steps, requests, model = tokens.shape
    width = input_weight.shape[2]
    units = expand_weight.shape[1]
    slots = key_cache.shape[1]
    rows = steps * requests
    shards = 2 * side * side
    wide_d = -(-model // 128) * 128
    cfg = (side, planes, steps, requests, slots, width, model, units)
    args = (
        tokens,
        first_gain,
        first_shift,
        input_weight.transpose(1, 0, 2),
        input_bias,
        output_weight.T,
        output_bias,
        second_gain,
        second_shift,
        expand_weight.T,
        expand_bias,
        contract_weight,
        contract_bias,
        key_cache,
        value_cache,
        cache_fill,
        owner_shard,
    )
    row = pltpu.VMEM((model,), F32)
    outs = (tokens.shape, key_cache.shape, value_cache.shape)
    results = pl.pallas_call(
        functools.partial(layer_kernel, cfg),
        out_shape=tuple(pltpu.VMEM(shape, BF16) for shape in outs),
        in_specs=[pl.BlockSpec(memory_space=pl.ANY)] * len(args),
        out_specs=tuple(pl.BlockSpec(memory_space=pltpu.VMEM) for _ in outs),
        scratch_shapes=[
            pltpu.VMEM(tokens.shape, BF16),
            row,
            row,
            pltpu.VMEM((3, model, width), BF16),
            pltpu.VMEM((3, width), F32),
            pltpu.VMEM((model, width), BF16),
            row,
            row,
            row,
            pltpu.VMEM((units, model), BF16),
            pltpu.VMEM((units,), F32),
            pltpu.VMEM((units, model), BF16),
            row,
            pltpu.SMEM(cache_fill.shape, jnp.int32),
            pltpu.SMEM(owner_shard.shape, jnp.int32),
            pltpu.VMEM((rows, model), F32),
            pltpu.VMEM((rows, width), F32),
            pltpu.VMEM((rows, width), F32),
            pltpu.VMEM((rows, 1, width + 128), F32),
            pltpu.VMEM((shards, 1, width + 128), F32),
            pltpu.VMEM((1, 1, wide_d), F32),
            pltpu.VMEM((planes, 1, wide_d), F32),
            pltpu.VMEM((1, 1, wide_d), F32),
            pltpu.VMEM((planes, 1, wide_d), F32),
            pltpu.VMEM((1, 1, wide_d), F32),
            pltpu.VMEM((rows, 1, wide_d), F32),
            pltpu.SemaphoreType.DMA((18,)),
            pltpu.SemaphoreType.DMA((4,)),
            pltpu.SemaphoreType.DMA((4,)),
        ],
        compiler_params=pltpu.CompilerParams(collective_id=0, has_side_effects=True),
        name="layer",
    )(*args)
    return pl.pallas_call(
        write_kernel,
        out_shape=tuple(jax.ShapeDtypeStruct(shape, BF16) for shape in outs),
        in_specs=[pl.BlockSpec(memory_space=pltpu.VMEM)] * len(outs),
        out_specs=tuple(pl.BlockSpec(memory_space=pl.ANY) for _ in outs),
        scratch_shapes=[pltpu.SemaphoreType.DMA((len(outs),))],
        name="write",
    )(*(pltpu.with_memory_space_constraint(r, pltpu.VMEM) for r in results))


def solution(mesh):
    side = math.isqrt(mesh.shape["seq"] // 2)
    return jax.shard_map(
        functools.partial(per_device, side, mesh.shape["tensor"]),
        mesh=mesh,
        in_specs=(
            P(),
            P(),
            P(),
            P(None, None, "tensor"),
            P(None, "tensor"),
            P("tensor", None),
            P(),
            P(),
            P(),
            P(None, "tensor"),
            P("tensor"),
            P("tensor", None),
            P(),
            P(None, "seq", "tensor"),
            P(None, "seq", "tensor"),
            P(),
            P(),
        ),
        out_specs=(P(), P(None, "seq", "tensor"), P(None, "seq", "tensor")),
        check_vma=False,
    )
```
